32 devices in a mesh: groups: 2 (over x), chan: 8 (over z, y), seq: 2 (over core).
Axes of the slice: x: 2, y: 2, z: 4, core: 2. Of those that a mesh axis runs over, the one named last changes fastest.
Arguments:
- tokens: bfloat16 [2048, 8192], P(('groups', 'seq'), 'chan'), parts along dimension 0, may hold values from -42 to 42
- norm_gain: float32 [8192], replicated, may hold values from 0.1 to 1.9
- in_weight: bfloat16 [3, 8192, 8192], P(None, None, 'chan'), may hold values from -0.0625 to 0.0625
- short_weight: float32 [3, 7, 8192], P(None, None, 'chan'), may hold values from -2 to 2
- log_decay: float32 [16, 8192], P(None, 'chan'), may hold values from -0.034 to 0
- residue: float32 [16, 8192], P(None, 'chan'), may hold values from -0.15625 to 0.15625
- skip: float32 [8192], P('chan'), may hold values from 0.1 to 1.9
- out_weight: bfloat16 [8192, 8192], P('chan'), may hold values from -0.09375 to 0.09375
Outputs:
- mixed: bfloat16 [2048, 8192], P(('groups', 'seq'), 'chan'), parts along dimension 0
The draws below stay inside these ranges and needn't reach their ends.
There are 2 independent parts, one for each index of `groups`. The reference program is written for one: setup_inputs(seed, part) draws one part's arguments, and reference() takes and returns one part's arrays. A program takes and returns all parts, laid end to end along the dimension named above; an argument that names none is the same for every part. Nothing has to cross between parts.
All inputs are finite; a program needn't handle non-finite values.
Results may differ from the reference program's by a relative error of at most 0.0067.
Values may be sent and summed in bfloat16 or wider, within the bound.
A program may use at most 448 MiB of HBM per device.

```python
import math
import jax
import jax.numpy as jnp
from jax import lax

D = 8192
POLES = 16
SHORT = 7
SEQ_LEN = 1024


def draw_tokens(key, part):
    keys = jax.random.split(key, 3)
    row_scale = jnp.exp(jax.random.uniform(keys[1], (SEQ_LEN, 1), jnp.float32, math.log(0.3), math.log(3.0)))
    ramp = jnp.sqrt(1.0 + 2.0 * jnp.arange(D, dtype=jnp.float32) / D)
    col_scale = jnp.exp(jax.random.uniform(keys[2], (1, D), jnp.float32, math.log(0.5), math.log(2.0))) * ramp[None, :]
    base = jnp.clip(jax.random.normal(keys[0], (SEQ_LEN, D), jnp.float32), -4.0, 4.0)
    return (base * row_scale * col_scale).astype(jnp.bfloat16)


def draw_log_decay(key, part):
    keys = jax.random.split(key, 3)
    slow = jnp.exp(jax.random.uniform(keys[0], (POLES, D), jnp.float32, math.log(0.1 / SEQ_LEN), math.log(2.0 / SEQ_LEN)))
    fast = jnp.exp(jax.random.uniform(keys[1], (POLES, D), jnp.float32, math.log(1.0 / 50.0), math.log(1.0 / 30.0)))
    share = 0.5
    picked = jax.random.uniform(keys[2], (POLES, D), jnp.float32) < share
    return -jnp.where(picked, fast, slow)


def with_spikes(drawn, own_key, source, target, shards_of, factor):
    def block_of(dim):
        return (jnp.arange(drawn.shape[dim]) // (drawn.shape[dim] // shards_of)).reshape((-1,) + (1,) * (drawn.ndim - 1 - dim))

    near = jax.random.permutation(own_key, shards_of)[block_of(target)]
    second = (block_of(target) + shards_of // 2) % shards_of
    return jnp.where((block_of(source) == near) | (block_of(source) == second), factor * drawn, drawn)


def block_levels(own_key, shape, shards, smallest, largest):
    factor_of = 1.0
    for dim, blocks in shards:
        steps = jax.random.uniform(jax.random.fold_in(jax.random.fold_in(own_key, 6), dim), (blocks,), jnp.float32, smallest / len(shards), largest / len(shards))
        factor_of = factor_of * jnp.repeat(jnp.exp(steps), shape[dim] // blocks).reshape((-1,) + (1,) * (len(shape) - 1 - dim))
    return factor_of


def gaussian(key, extent, spread, reach, shards=(), kind=jnp.bfloat16):
    values = spread * jax.random.normal(key, extent, jnp.float32)
    if shards:
        values = values * block_levels(key, extent, shards, -0.22, 0.18)
    return jnp.clip(values, -reach, reach).astype(kind)


def noise_with(key, extent, spread, most, cuts, heavy, held_as=jnp.bfloat16):
    array = spread * jax.random.normal(key, extent, jnp.float32)
    if cuts:
        array = array * block_levels(key, extent, cuts, -0.22, 0.18)
    return jnp.clip(with_spikes(array, jax.random.fold_in(key, 3), *heavy), -most, most).astype(held_as)


def setup_inputs(seed: int = 0, part: int = 0) -> dict:
    splits = jax.random.split(jax.random.key(seed), 9)
    own_keys = jax.random.split(jax.random.fold_in(splits[8], part), 9)
    return {
        "tokens": draw_tokens(jax.random.fold_in(jax.random.fold_in(splits[8], part), 71), part),
        "norm_gain": jnp.clip(1.0 + 0.18 * jax.random.normal(splits[1], (D,), jnp.float32), 0.1, 1.9),
        "in_weight": gaussian(splits[2], (3, D, D), D ** -0.5, 0.0625, ((2, 8),)),
        "short_weight": gaussian(splits[3], (3, SHORT, D), SHORT ** -0.5, 2.0, ((2, 8),), jnp.float32),
        "log_decay": draw_log_decay(jax.random.fold_in(splits[8], 71), part),
        "residue": gaussian(splits[5], (POLES, D), ((2.0 / (POLES * SEQ_LEN)) ** 0.5), 0.15625, ((1, 8),), jnp.float32),
        "skip": jnp.clip(1.0 + 0.18 * jax.random.normal(splits[6], (D,), jnp.float32), 0.1, 1.9),
        "out_weight": noise_with(splits[7], (D, D), D ** -0.5, 0.09375, ((0, 8),), (0, 1, 8, 2.0)),
    }


EPSILON = 1e-06

def reference(tokens, norm_gain, in_weight, short_weight, log_decay, residue, skip, out_weight):
    seq_total = tokens.shape[0]
    taps = short_weight.shape[1]
    tok_float = tokens.astype(jnp.float32)
    inv_rms = lax.rsqrt(lax.optimization_barrier(jnp.mean(tok_float * tok_float, axis=1, keepdims=True)) + EPSILON)
    scaled = (tok_float * norm_gain[None, :]).astype(jnp.bfloat16)
    proj = jnp.stack([(jnp.dot(scaled, in_weight[which], preferred_element_type=jnp.float32) * inv_rms).astype(jnp.bfloat16) for which in range(3)])
    proj_float = proj.astype(jnp.float32)
    padded = jnp.pad(proj_float, ((0, 0), (taps - 1, 0), (0, 0)))
    conv = jnp.zeros_like(proj_float)
    for tap in range(taps):
        conv = conv + short_weight[:, tap][:, None, :] * padded[:, taps - 1 - tap:taps - 1 - tap + seq_total, :]
    query = conv[0]
    product = conv[1] * conv[2]
    poles = jnp.exp(log_decay)

    def advance(state, row):
        state = poles * state + row[None, :]
        return (state, lax.optimization_barrier(jnp.sum(residue * state, axis=0)))
    _, long_conv = lax.scan(advance, jnp.zeros(log_decay.shape, jnp.float32), product)
    gated = (query * (long_conv + skip[None, :] * product)).astype(jnp.bfloat16)
    return (tok_float + jnp.dot(gated, out_weight, preferred_element_type=jnp.float32)).astype(jnp.bfloat16)
```

```python
import functools

import jax
import jax.numpy as jnp
from jax import lax
from jax.experimental import pallas as pl
from jax.experimental.pallas import tpu as pltpu
from jax.sharding import PartitionSpec as P

EPSILON = 1e-06
MESH = pl.DeviceIdType.MESH
PIECES = 2
W_SLOTS = 4


def ring_position(index, n):
    odd = lax.rem(index, 2)
    return (1 - odd) * lax.div(index, 2) + odd * (n - 1 - lax.div(index, 2))


def ring_index(position, n):
    back = lax.div(position, n // 2)
    return (1 - back) * (2 * position) + back * (2 * (n - 1 - position) + 1)


def greet(peers):
    barrier = pltpu.get_barrier_semaphore()
    for peer in peers:
        pl.semaphore_signal(barrier, inc=1, device_id=peer, device_id_type=MESH)
    pl.semaphore_wait(barrier, len(peers))


def strided(start, size, stride):
    return pl.ds(start, size) if stride == 1 else pl.ds(start, size, stride=stride)


def front_kernel(
    n, eps, tok_hbm, gain_ref, w_hbm, taps_ref, decay_ref, res_ref, skip_ref, gated_ref,
    held, acc, w_buf, scaled, squares, query, signal_rows, pole, residue, skip_rows,
    rim_out, rim_in, state_out, state_in, send_sem, recv_sem, w_sem, own_sem, pair_send, pair_recv,
):
    rows, width = tok_hbm.shape
    half = rows // 2
    piece = half // PIECES
    groups = width // 128
    poles = decay_ref.shape[0]
    tap_count = taps_ref.shape[1]
    chunk = min(64, half)
    tile = min(256, width)
    me = lax.axis_index("chan")
    seq = lax.axis_index("seq")
    pos = ring_position(me, n)
    right = {"chan": ring_index(lax.rem(pos + 1, n), n)}
    left = {"chan": ring_index(lax.rem(pos + n - 1, n), n)}
    partner = {"seq": 1 - seq}
    ahead = (right, left)

    def owner_of(direction, step):
        shift = lax.rem(pos + n - step, n) if direction == 0 else lax.rem(pos + step, n)
        return ring_index(shift, n)

    def owner_dyn(direction, step):
        return ring_index(lax.rem(pos + (1 - direction) * (n - step) + direction * step, n), n)

    def w_copy(g):
        unit = lax.div(g, 3)
        owner = owner_dyn(lax.rem(unit, 2), lax.div(unit, 2))
        slot = lax.rem(g, W_SLOTS)
        return pltpu.make_async_copy(
            w_hbm.at[lax.rem(g, 3), pl.ds(pl.multiple_of(owner * width, 128), width), :],
            w_buf.at[slot],
            w_sem.at[slot],
        )

    def hop(direction, step, part, block_step):
        owner = owner_of(direction, block_step)
        span = pl.ds(direction * half + part * piece, piece)
        return pltpu.make_async_remote_copy(
            src_ref=held.at[owner, span, :],
            dst_ref=held.at[owner, span, :],
            send_sem=send_sem.at[direction, step, part],
            recv_sem=recv_sem.at[direction, step, part],
            device_id=ahead[direction],
            device_id_type=MESH,
        )

    own = pltpu.make_async_copy(tok_hbm, held.at[me], own_sem)
    own.start()
    for g in range(W_SLOTS):
        w_copy(jnp.int32(g)).start()
    greet((right, left, partner))
    own.wait()
    for part in range(PIECES):
        for direction in range(2):
            hop(direction, 0, part, 0).start()

    @pl.loop(0, rows // chunk)
    def _(b):
        r = pl.multiple_of(b * chunk, chunk)
        squares[pl.ds(r, chunk), :] = jnp.zeros((chunk, 128), jnp.float32)
        for i in range(3):
            acc[i, pl.ds(r + 8, chunk), :] = jnp.zeros((chunk, width), jnp.float32)

    for j in range(groups):
        lanes = pl.ds(j * 128, 128)
        pole[strided(j, poles, groups), :] = jnp.exp(decay_ref[:, lanes])
        residue[strided(j, poles, groups), :] = res_ref[:, lanes]
        skip_rows[pl.ds(j, 1), :] = skip_ref[:, lanes]

    def compute(step, direction):
        owner = owner_of(direction, step)
        first = direction * half
        gain = gain_ref[:, pl.ds(pl.multiple_of(owner * width, 128), width)]
        small = min(32, half)

        @pl.loop(0, half // small)
        def _(b):
            r = pl.multiple_of(b * small, small)
            x = held[owner, pl.ds(first + r, small), :].astype(jnp.float32)
            scaled[pl.ds(r, small), :] = (x * gain).astype(jnp.bfloat16)
            total = squares[pl.ds(first + r, small), :]
            for j in range(groups):
                xj = x[:, j * 128 : (j + 1) * 128]
                total = total + xj * xj
            squares[pl.ds(first + r, small), :] = total

        @pl.loop(0, 3)
        def _(i):
            g = (step * 2 + direction) * 3 + i
            slot = lax.rem(g, W_SLOTS)
            w_copy(g).wait()

            @pl.loop(0, width // tile)
            def _(c):
                cols = pl.ds(pl.multiple_of(c * tile, 128), tile)
                acc[i, pl.ds(first + 8, half), cols] += jnp.dot(
                    scaled[...], w_buf[slot, :, cols], preferred_element_type=jnp.float32
                )

            @pl.when(g + W_SLOTS < n * 6)
            def _():
                w_copy(g + W_SLOTS).start()

    @pl.loop(1, n)
    def _(step):
        for part in range(PIECES):
            for direction in range(2):
                hop(direction, step - 1, part, step).wait_recv()

                @pl.when(step < n - 1)
                def _():
                    hop(direction, step, part, step).start()

            compute(step - 1, part)

    @pl.loop(n - 1, n)
    def _(step):
        for direction in range(2):
            compute(step, direction)

    @pl.loop(0, rows // chunk)
    def _(b):
        r = pl.multiple_of(b * chunk, chunk)
        mean = jnp.sum(squares[pl.ds(r, chunk), :], axis=1, keepdims=True) / (n * width)
        inv = lax.rsqrt(mean + eps)
        for i in range(3):
            span = pl.ds(r + 8, chunk)
            acc[i, span, :] = (acc[i, span, :] * inv).astype(jnp.bfloat16).astype(jnp.float32)

    rim_out[...] = acc[:, pl.ds(rows, 8), :]
    rim = pltpu.make_async_remote_copy(
        src_ref=rim_out, dst_ref=rim_in, send_sem=pair_send.at[0], recv_sem=pair_recv.at[0],
        device_id=partner, device_id_type=MESH,
    )
    rim.start()
    rim.wait()
    acc[:, pl.ds(0, 8), :] = jnp.where(seq > 0, rim_in[...], 0.0)

    @pl.loop(0, groups)
    def _(j):
        lanes = pl.ds(pl.multiple_of(j * 128, 128), 128)

        @pl.loop(0, rows // chunk)
        def _(b):
            r = pl.multiple_of(b * chunk, chunk)
            conv = []
            for i in range(3):
                x = acc[i, pl.ds(r, chunk + 8), lanes]
                total = x[8:, :] * taps_ref[i, pl.ds(0, 1), lanes]
                for tap in range(1, tap_count):
                    shifted = pltpu.roll(x, tap, 0)[8:, :]
                    total = total + shifted * taps_ref[i, pl.ds(tap, 1), lanes]
                conv.append(total)
            query[pl.ds(r, chunk), lanes] = conv[0]
            signal_rows[strided(r * groups + j, chunk, groups), :] = conv[1] * conv[2]

    def row_at(t):
        return pl.ds(pl.multiple_of(t * groups, groups), groups)

    poles_held = [pole[pl.ds(k * groups, groups), :] for k in range(poles)]

    def only_state(t, state):
        row = signal_rows[row_at(t), :]
        return tuple(poles_held[k] * state[k] + row for k in range(poles))

    zero = tuple(jnp.zeros((groups, 128), jnp.float32) for _ in range(poles))
    last = lax.fori_loop(0, rows, only_state, zero, unroll=8)
    for k in range(poles):
        state_out[pl.ds(k * groups, groups), :] = last[k]
    carry = pltpu.make_async_remote_copy(
        src_ref=state_out, dst_ref=state_in, send_sem=pair_send.at[1], recv_sem=pair_recv.at[1],
        device_id=partner, device_id_type=MESH,
    )
    carry.start()
    carry.wait()
    res_held = [residue[pl.ds(k * groups, groups), :] for k in range(poles)]
    skip_held = skip_rows[...]

    def with_output(t, state):
        row = signal_rows[row_at(t), :]
        state = tuple(poles_held[k] * state[k] + row for k in range(poles))
        terms = [res_held[k] * state[k] for k in range(poles)]
        while len(terms) > 1:
            terms = [a + b for a, b in zip(terms[::2], terms[1::2])] + terms[len(terms) // 2 * 2 :]
        signal_rows[row_at(t), :] = terms[0] + skip_held * row
        return state

    entry = tuple(
        jnp.where(seq > 0, state_in[pl.ds(k * groups, groups), :], 0.0) for k in range(poles)
    )
    lax.fori_loop(0, rows, with_output, entry, unroll=4)

    @pl.loop(0, groups)
    def _(j):
        lanes = pl.ds(pl.multiple_of(j * 128, 128), 128)

        @pl.loop(0, rows // chunk)
        def _(b):
            r = pl.multiple_of(b * chunk, chunk)
            long = signal_rows[strided(r * groups + j, chunk, groups), :]
            gated_ref[pl.ds(r, chunk), lanes] = (query[pl.ds(r, chunk), lanes] * long).astype(jnp.bfloat16)

    @pl.loop(0, n - 1)
    def _(step):
        for part in range(PIECES):
            for direction in range(2):
                hop(direction, step, part, step).wait_send()


def back_kernel(
    n, gated_ref, tok_ref, w_hbm, out_ref, w_buf, partial, outgoing, incoming, send_sem, recv_sem, w_sem
):
    rows, width = tok_ref.shape
    half = rows // 2
    piece = half // PIECES
    tile = min(256, width)
    me = lax.axis_index("chan")
    pos = ring_position(me, n)
    right = {"chan": ring_index(lax.rem(pos + 1, n), n)}
    left = {"chan": ring_index(lax.rem(pos + n - 1, n), n)}
    ahead = (right, left)

    def w_copy(direction, step):
        if direction == 0:
            target = ring_index(lax.rem(pos + 2 * n - 1 - step, n), n)
        else:
            target = ring_index(lax.rem(pos + 1 + step, n), n)
        slot = lax.rem(step, 2)
        return pltpu.make_async_copy(
            w_hbm.at[:, pl.ds(pl.multiple_of(target * width, 128), width)],
            w_buf.at[direction, slot],
            w_sem.at[direction, slot],
        )

    def hop(direction, step, part):
        span = pl.ds(part * piece, piece)
        return pltpu.make_async_remote_copy(
            src_ref=outgoing.at[direction, step, span, :],
            dst_ref=incoming.at[direction, step, span, :],
            send_sem=send_sem.at[direction, step, part],
            recv_sem=recv_sem.at[direction, step, part],
            device_id=ahead[direction],
            device_id_type=MESH,
        )

    def multiply(step):
        for direction in range(2):
            w_copy(direction, step).wait()
            slot = lax.rem(step, 2)

            @pl.loop(0, width // tile)
            def _(c):
                cols = pl.ds(pl.multiple_of(c * tile, 128), tile)
                partial[direction, :, cols] = jnp.dot(
                    gated_ref[pl.ds(direction * half, half), :],
                    w_buf[direction, slot, :, cols],
                    preferred_element_type=jnp.float32,
                )

            @pl.when(step + 2 < n)
            def _():
                w_copy(direction, step + 2).start()

    for step in range(2):
        for direction in range(2):
            w_copy(direction, jnp.int32(step)).start()
    greet((right, left))
    small = min(32, piece)
    multiply(jnp.int32(0))
    for part in range(PIECES):
        for direction in range(2):

            @pl.loop(0, piece // small)
            def _(b):
                r = pl.multiple_of(part * piece + b * small, small)
                outgoing[direction, 0, pl.ds(r, small), :] = partial[
                    direction, pl.ds(r, small), :
                ].astype(jnp.bfloat16)

            hop(direction, 0, part).start()

    @pl.loop(1, n - 1)
    def _(step):
        multiply(step)
        for part in range(PIECES):
            for direction in range(2):
                hop(direction, step - 1, part).wait_recv()

                @pl.loop(0, piece // small)
                def _(b):
                    r = pl.multiple_of(part * piece + b * small, small)
                    span = pl.ds(r, small)
                    outgoing[direction, step, span, :] = (
                        partial[direction, span, :]
                        + incoming[direction, step - 1, span, :].astype(jnp.float32)
                    ).astype(jnp.bfloat16)

                hop(direction, step, part).start()

    multiply(jnp.int32(n - 1))
    for part in range(PIECES):
        for direction in range(2):
            hop(direction, n - 2, part).wait_recv()

            @pl.loop(0, piece // small)
            def _(b):
                r = pl.multiple_of(part * piece + b * small, small)
                span = pl.ds(r, small)
                whole = pl.ds(direction * half + r, small)
                out_ref[whole, :] = (
                    tok_ref[whole, :].astype(jnp.float32)
                    + (
                        partial[direction, span, :]
                        + incoming[direction, n - 2, span, :].astype(jnp.float32)
                    )
                ).astype(jnp.bfloat16)

    @pl.loop(0, n - 1)
    def _(step):
        for part in range(PIECES):
            for direction in range(2):
                hop(direction, step, part).wait_send()


def per_device(n, tokens, norm_gain, in_weight, short_weight, log_decay, residue, skip, out_weight):
    rows, width = tokens.shape
    groups = width // 128
    poles = log_decay.shape[0]
    half = rows // 2
    vmem = pl.BlockSpec(memory_space=pltpu.VMEM)
    anywhere = pl.BlockSpec(memory_space=pl.ANY)
    f32, bf16 = jnp.float32, jnp.bfloat16
    dma = pltpu.SemaphoreType.DMA
    gated = pl.pallas_call(
        functools.partial(front_kernel, n, EPSILON),
        out_shape=jax.ShapeDtypeStruct((rows, width), bf16),
        in_specs=[anywhere, vmem, anywhere, vmem, vmem, vmem, vmem],
        out_specs=vmem,
        scratch_shapes=[
            pltpu.VMEM((n, rows, width), bf16),
            pltpu.VMEM((3, rows + 8, width), f32),
            pltpu.VMEM((W_SLOTS, width, width), bf16),
            pltpu.VMEM((half, width), bf16),
            pltpu.VMEM((rows, 128), f32),
            pltpu.VMEM((rows, width), f32),
            pltpu.VMEM((rows * groups, 128), f32),
            pltpu.VMEM((poles * groups, 128), f32),
            pltpu.VMEM((poles * groups, 128), f32),
            pltpu.VMEM((groups, 128), f32),
            pltpu.VMEM((3, 8, width), f32),
            pltpu.VMEM((3, 8, width), f32),
            pltpu.VMEM((poles * groups, 128), f32),
            pltpu.VMEM((poles * groups, 128), f32),
            dma((2, n - 1, PIECES)),
            dma((2, n - 1, PIECES)),
            dma((W_SLOTS,)),
            dma,
            dma((2,)),
            dma((2,)),
        ],
        compiler_params=pltpu.CompilerParams(
            collective_id=0, has_side_effects=True, vmem_limit_bytes=56 << 20
        ),
    )(tokens, norm_gain[None, :], in_weight, short_weight, log_decay, residue, skip[None, :])
    return pl.pallas_call(
        functools.partial(back_kernel, n),
        out_shape=jax.ShapeDtypeStruct((rows, width), bf16),
        in_specs=[vmem, vmem, anywhere],
        out_specs=vmem,
        scratch_shapes=[
            pltpu.VMEM((2, 2, width, width), bf16),
            pltpu.VMEM((2, half, width), f32),
            pltpu.VMEM((2, n - 1, half, width), bf16),
            pltpu.VMEM((2, n - 1, half, width), bf16),
            dma((2, n - 1, PIECES)),
            dma((2, n - 1, PIECES)),
            dma((2, 2)),
        ],
        compiler_params=pltpu.CompilerParams(
            collective_id=1, has_side_effects=True, vmem_limit_bytes=56 << 20
        ),
    )(gated, tokens, out_weight)


def solution(mesh):
    return jax.shard_map(
        functools.partial(per_device, mesh.shape["chan"]),
        mesh=mesh,
        in_specs=(
            P(("groups", "seq"), "chan"),
            P(),
            P(None, None, "chan"),
            P(None, None, "chan"),
            P(None, "chan"),
            P(None, "chan"),
            P("chan"),
            P("chan", None),
        ),
        out_specs=P(("groups", "seq"), "chan"),
        check_vma=False,
    )
```

```python
import functools

import jax
import jax.numpy as jnp
from jax import lax
from jax.experimental import pallas as pl
from jax.experimental.pallas import tpu as pltpu
from jax.sharding import PartitionSpec as P

EPSILON = 1e-06
MESH = pl.DeviceIdType.MESH
PIECES = 4
W_SLOTS = 4


def ring_position(index, n):
    odd = lax.rem(index, 2)
    return (1 - odd) * lax.div(index, 2) + odd * (n - 1 - lax.div(index, 2))


def ring_index(position, n):
    back = lax.div(position, n // 2)
    return (1 - back) * (2 * position) + back * (2 * (n - 1 - position) + 1)


def greet(peers):
    barrier = pltpu.get_barrier_semaphore()
    for peer in peers:
        pl.semaphore_signal(barrier, inc=1, device_id=peer, device_id_type=MESH)
    pl.semaphore_wait(barrier, len(peers))


def strided(start, size, stride):
    return pl.ds(start, size) if stride == 1 else pl.ds(start, size, stride=stride)


def front_kernel(
    n, eps, tok_hbm, gain_ref, w_hbm, taps_ref, decay_ref, res_ref, skip_ref, gated_ref,
    held, acc, w_buf, scaled, squares, query, signal_rows, pole, residue, skip_rows,
    rim_out, rim_in, state_out, state_in, first_state, send_sem, recv_sem, w_sem, own_sem, pair_send, pair_recv, turn,
):
    rows, width = tok_hbm.shape
    middle = n // 2
    piece = rows // PIECES
    groups = width // 128
    poles = decay_ref.shape[0]
    tap_count = taps_ref.shape[1]
    chunk = min(64, rows)
    tile = min(256, width)
    me = lax.axis_index("chan")
    seq = lax.axis_index("seq")
    pos = ring_position(me, n)
    right = {"chan": ring_index(lax.rem(pos + 1, n), n)}
    left = {"chan": ring_index(lax.rem(pos + n - 1, n), n)}
    partner = {"seq": 1 - seq}
    ahead = (right, left)

    def owner_of(block):
        away = lax.div(block + 1, 2)
        odd = lax.rem(block, 2)
        return ring_index(lax.rem(pos + odd * (n - away) + (1 - odd) * away, n), n)

    def w_copy(g):
        owner = owner_of(lax.div(g, 3))
        slot = lax.rem(g, W_SLOTS)
        return pltpu.make_async_copy(
            w_hbm.at[lax.rem(g, 3), pl.ds(pl.multiple_of(owner * width, 128), width), :],
            w_buf.at[slot],
            w_sem.at[slot],
        )

    def hop(direction, step, part, away):
        shift = pos + n - away if direction == 0 else pos + away
        owner = ring_index(lax.rem(shift, n), n)
        span = pl.ds(part * piece, piece)
        return pltpu.make_async_remote_copy(
            src_ref=held.at[owner, span, :],
            dst_ref=held.at[owner, span, :],
            send_sem=send_sem.at[direction, step, part],
            recv_sem=recv_sem.at[direction, step, part],
            device_id=ahead[direction],
            device_id_type=MESH,
        )

    own = pltpu.make_async_copy(tok_hbm, held.at[me], own_sem)
    own.start()
    for g in range(W_SLOTS):
        w_copy(jnp.int32(g)).start()
    greet((right, left, partner))
    own.wait()

    @pl.when(seq > 0)
    def _():
        pl.semaphore_wait(turn, 1)

    for part in range(PIECES):
        for direction in range(2):
            hop(direction, 0, part, 0).start()

    @pl.loop(0, rows // chunk)
    def _(b):
        r = pl.multiple_of(b * chunk, chunk)
        squares[pl.ds(r, chunk), :] = jnp.zeros((chunk, 128), jnp.float32)
        for i in range(3):
            acc[i, pl.ds(r + 8, chunk), :] = jnp.zeros((chunk, width), jnp.float32)

    for j in range(groups):
        lanes = pl.ds(j * 128, 128)
        pole[strided(j, poles, groups), :] = jnp.exp(decay_ref[:, lanes])
        residue[strided(j, poles, groups), :] = res_ref[:, lanes]
        skip_rows[pl.ds(j, 1), :] = skip_ref[:, lanes]

    def prepare(block):
        owner = owner_of(block)
        gain = gain_ref[:, pl.ds(pl.multiple_of(owner * width, 128), width)]
        small = min(32, rows)

        @pl.loop(0, rows // small)
        def _(b):
            r = pl.multiple_of(b * small, small)
            x = held[owner, pl.ds(r, small), :].astype(jnp.float32)
            scaled[pl.ds(r, small), :] = (x * gain).astype(jnp.bfloat16)
            total = squares[pl.ds(r, small), :]
            for j in range(groups):
                xj = x[:, j * 128 : (j + 1) * 128]
                total = total + xj * xj
            squares[pl.ds(r, small), :] = total

    def multiply(block, i):
        g = block * 3 + i
        slot = lax.rem(g, W_SLOTS)
        w_copy(g).wait()

        @pl.loop(0, width // tile)
        def _(c):
            cols = pl.ds(pl.multiple_of(c * tile, 128), tile)
            acc[i, pl.ds(8, rows), cols] += jnp.dot(
                scaled[...], w_buf[slot, :, cols], preferred_element_type=jnp.float32
            )

        @pl.when(g + W_SLOTS < n * 3)
        def _():
            w_copy(g + W_SLOTS).start()

    def arrive(step, part):
        for direction in range(2):
            hop(direction, step - 1, part, step).wait_recv()
            if part // (PIECES // 2) == direction:
                hop(direction, step, part, step).start()
            else:

                @pl.when(step < middle - 1)
                def _():
                    hop(direction, step, part, step).start()

    def pair_part(step, quarter):
        near = 2 * step - 1
        if quarter == 0:
            prepare(near)
            multiply(near, 0)
            multiply(near, 1)
        elif quarter == 1:
            multiply(near, 2)
        elif quarter == 2:
            prepare(near + 1)
            multiply(near + 1, 0)
            multiply(near + 1, 1)
        else:
            multiply(near + 1, 2)

    for part in range(PIECES):
        arrive(jnp.int32(1), part)
        if part == 0:
            prepare(jnp.int32(0))
        if part < 3:
            multiply(jnp.int32(0), part)

    @pl.loop(2, middle)
    def _(step):
        for part in range(PIECES):
            arrive(step, part)
            pair_part(step - 1, part)

    @pl.when(seq == 0)
    def _():
        pl.semaphore_signal(turn, inc=1, device_id=partner, device_id_type=MESH)

    for part in range(PIECES):
        pair_part(jnp.int32(middle - 1), part)
    for part in range(PIECES):
        hop(part // (PIECES // 2), middle - 1, part, middle).wait_recv()
    prepare(jnp.int32(n - 1))
    for i in range(3):
        multiply(jnp.int32(n - 1), i)

    @pl.loop(0, rows // chunk)
    def _(b):
        r = pl.multiple_of(b * chunk, chunk)
        mean = jnp.sum(squares[pl.ds(r, chunk), :], axis=1, keepdims=True) / (n * width)
        inv = lax.rsqrt(mean + eps)
        for i in range(3):
            span = pl.ds(r + 8, chunk)
            acc[i, span, :] = (acc[i, span, :] * inv).astype(jnp.bfloat16).astype(jnp.float32)

    rim_out[...] = acc[:, pl.ds(rows, 8), :]
    rim = pltpu.make_async_remote_copy(
        src_ref=rim_out, dst_ref=rim_in, send_sem=pair_send.at[0], recv_sem=pair_recv.at[0],
        device_id=partner, device_id_type=MESH,
    )

    @pl.when(seq == 0)
    def _():
        rim.start()

    @pl.when(seq > 0)
    def _():
        rim.wait_recv()

    acc[:, pl.ds(0, 8), :] = jnp.zeros((3, 8, width), jnp.float32)

    @pl.when(seq > 0)
    def _():
        acc[:, pl.ds(0, 8), :] = rim_in[...]


    @pl.loop(0, groups)
    def _(j):
        lanes = pl.ds(pl.multiple_of(j * 128, 128), 128)

        @pl.loop(0, rows // chunk)
        def _(b):
            r = pl.multiple_of(b * chunk, chunk)
            conv = []
            for i in range(3):
                x = acc[i, pl.ds(r, chunk + 8), lanes]
                total = x[8:, :] * taps_ref[i, pl.ds(0, 1), lanes]
                for tap in range(1, tap_count):
                    shifted = pltpu.roll(x, tap, 0)[8:, :]
                    total = total + shifted * taps_ref[i, pl.ds(tap, 1), lanes]
                conv.append(total)
            query[pl.ds(r, chunk), lanes] = conv[0]
            signal_rows[strided(r * groups + j, chunk, groups), :] = conv[1] * conv[2]

    def row_at(t):
        return pl.ds(pl.multiple_of(t * groups, groups), groups)

    poles_held = [pole[pl.ds(k * groups, groups), :] for k in range(poles)]

    carry = pltpu.make_async_remote_copy(
        src_ref=state_out, dst_ref=state_in, send_sem=pair_send.at[1], recv_sem=pair_recv.at[1],
        device_id=partner, device_id_type=MESH,
    )
    entry_rows = poles * groups

    @pl.when(seq == 0)
    def _():
        first_state[...] = jnp.zeros((entry_rows, 128), jnp.float32)

    @pl.when(seq > 0)
    def _():
        carry.wait_recv()
        first_state[...] = state_in[...]

    res_held = [residue[pl.ds(k * groups, groups), :] for k in range(poles)]
    skip_held = skip_rows[...]

    def with_output(t, state):
        row = signal_rows[row_at(t), :]
        state = tuple(poles_held[k] * state[k] + row for k in range(poles))
        terms = [res_held[k] * state[k] for k in range(poles)]
        while len(terms) > 1:
            terms = [a + b for a, b in zip(terms[::2], terms[1::2])] + terms[len(terms) // 2 * 2 :]
        signal_rows[row_at(t), :] = terms[0] + skip_held * row
        return state

    entry = tuple(first_state[pl.ds(k * groups, groups), :] for k in range(poles))
    last = lax.fori_loop(0, rows, with_output, entry, unroll=4)
    for k in range(poles):
        state_out[pl.ds(k * groups, groups), :] = last[k]

    @pl.when(seq == 0)
    def _():
        carry.start()

    @pl.loop(0, groups)
    def _(j):
        lanes = pl.ds(pl.multiple_of(j * 128, 128), 128)

        @pl.loop(0, rows // chunk)
        def _(b):
            r = pl.multiple_of(b * chunk, chunk)
            long = signal_rows[strided(r * groups + j, chunk, groups), :]
            gated_ref[pl.ds(r, chunk), lanes] = (query[pl.ds(r, chunk), lanes] * long).astype(jnp.bfloat16)

    @pl.when(seq == 0)
    def _():
        rim.wait_send()
        carry.wait_send()

    for part in range(PIECES):
        for direction in range(2):

            @pl.loop(0, middle - 1)
            def _(step):
                hop(direction, step, part, step).wait_send()

        hop(part // (PIECES // 2), middle - 1, part, middle - 1).wait_send()


def back_kernel(
    n, gated_ref, tok_ref, w_hbm, out_ref, w_buf, partial, outgoing, incoming, send_sem, recv_sem, w_sem
):
    rows, width = tok_ref.shape
    middle = n // 2
    piece = rows // PIECES
    small = min(32, piece)
    tile = min(256, width)
    me = lax.axis_index("chan")
    pos = ring_position(me, n)
    right = {"chan": ring_index(lax.rem(pos + 1, n), n)}
    left = {"chan": ring_index(lax.rem(pos + n - 1, n), n)}
    ahead = (right, left)

    def w_copy(block):
        away = middle - lax.div(block + 1, 2)
        odd = lax.rem(block, 2)
        target = ring_index(lax.rem(pos + odd * away + (1 - odd) * (n - away), n), n)
        slot = lax.rem(block, W_SLOTS)
        return pltpu.make_async_copy(
            w_hbm.at[:, pl.ds(pl.multiple_of(target * width, 128), width)],
            w_buf.at[slot],
            w_sem.at[slot],
        )

    def hop(direction, step, part):
        span = pl.ds(part * piece, piece)
        return pltpu.make_async_remote_copy(
            src_ref=outgoing.at[direction, step, span, :],
            dst_ref=incoming.at[direction, step, span, :],
            send_sem=send_sem.at[direction, step, part],
            recv_sem=recv_sem.at[direction, step, part],
            device_id=ahead[direction],
            device_id_type=MESH,
        )

    def multiply(block, place):
        slot = lax.rem(block, W_SLOTS)
        w_copy(block).wait()

        @pl.loop(0, width // tile)
        def _(c):
            cols = pl.ds(pl.multiple_of(c * tile, 128), tile)
            partial[place, :, cols] = jnp.dot(
                gated_ref[...], w_buf[slot, :, cols], preferred_element_type=jnp.float32
            )

        @pl.when(block + W_SLOTS < n)
        def _():
            w_copy(block + W_SLOTS).start()

    def send(direction, step, part, place, add):
        @pl.loop(0, piece // small)
        def _(b):
            span = pl.ds(pl.multiple_of(part * piece + b * small, small), small)
            total = partial[place, span, :]
            if add:
                total = total + incoming[direction, step - 1, span, :].astype(jnp.float32)
            outgoing[direction, step, span, :] = total.astype(jnp.bfloat16)

        hop(direction, step, part).start()

    def side(part):
        return part // (PIECES // 2)

    order = [k // 2 + (k % 2) * (PIECES // 2) for k in range(PIECES)]
    for block in range(W_SLOTS):
        w_copy(jnp.int32(block)).start()
    greet((right, left))
    multiply(jnp.int32(0), 0)
    for part in order:
        send(side(part), 0, part, 0, False)
    for direction in range(2):
        multiply(jnp.int32(1 + direction), direction)
    for direction in range(2):
        for part in range(PIECES):
            if side(part) != direction:
                send(direction, 1, part, direction, False)
    for part in order:
        hop(side(part), 0, part).wait_recv()
        send(side(part), 1, part, side(part), True)

    @pl.loop(2, middle)
    def _(step):
        for direction in range(2):
            multiply(2 * step - 1 + direction, direction)
        for k in range(PIECES):
            for direction in range(2):
                part = (k + (1 - direction) * (PIECES // 2)) % PIECES
                hop(direction, step - 1, part).wait_recv()
                send(direction, step, part, direction, True)

    multiply(jnp.int32(n - 1), 0)
    for part in range(PIECES):
        for direction in range(2):
            hop(direction, middle - 1, part).wait_recv()

        @pl.loop(0, piece // small)
        def _(b):
            span = pl.ds(pl.multiple_of(part * piece + b * small, small), small)
            total = partial[0, span, :]
            for direction in range(2):
                total = total + incoming[direction, middle - 1, span, :].astype(jnp.float32)
            out_ref[span, :] = (tok_ref[span, :].astype(jnp.float32) + total).astype(jnp.bfloat16)

    for part in range(PIECES):
        hop(side(part), 0, part).wait_send()
        for direction in range(2):

            @pl.loop(1, middle)
            def _(step):
                hop(direction, step, part).wait_send()


def per_device(n, tokens, norm_gain, in_weight, short_weight, log_decay, residue, skip, out_weight):
    rows, width = tokens.shape
    groups = width // 128
    poles = log_decay.shape[0]
    middle = n // 2
    vmem = pl.BlockSpec(memory_space=pltpu.VMEM)
    anywhere = pl.BlockSpec(memory_space=pl.ANY)
    f32, bf16 = jnp.float32, jnp.bfloat16
    dma = pltpu.SemaphoreType.DMA
    gated = pl.pallas_call(
        functools.partial(front_kernel, n, EPSILON),
        out_shape=jax.ShapeDtypeStruct((rows, width), bf16),
        in_specs=[anywhere, vmem, anywhere, vmem, vmem, vmem, vmem],
        out_specs=vmem,
        scratch_shapes=[
            pltpu.VMEM((n, rows, width), bf16),
            pltpu.VMEM((3, rows + 8, width), f32),
            pltpu.VMEM((W_SLOTS, width, width), bf16),
            pltpu.VMEM((rows, width), bf16),
            pltpu.VMEM((rows, 128), f32),
            pltpu.VMEM((rows, width), f32),
            pltpu.VMEM((rows * groups, 128), f32),
            pltpu.VMEM((poles * groups, 128), f32),
            pltpu.VMEM((poles * groups, 128), f32),
            pltpu.VMEM((groups, 128), f32),
            pltpu.VMEM((3, 8, width), f32),
            pltpu.VMEM((3, 8, width), f32),
            pltpu.VMEM((poles * groups, 128), f32),
            pltpu.VMEM((poles * groups, 128), f32),
            pltpu.VMEM((poles * groups, 128), f32),
            dma((2, middle, PIECES)),
            dma((2, middle, PIECES)),
            dma((W_SLOTS,)),
            dma,
            dma((2,)),
            dma((2,)),
            pltpu.SemaphoreType.REGULAR,
        ],
        compiler_params=pltpu.CompilerParams(
            collective_id=0, has_side_effects=True, vmem_limit_bytes=56 << 20
        ),
    )(tokens, norm_gain[None, :], in_weight, short_weight, log_decay, residue, skip[None, :])
    return pl.pallas_call(
        functools.partial(back_kernel, n),
        out_shape=jax.ShapeDtypeStruct((rows, width), bf16),
        in_specs=[vmem, vmem, anywhere],
        out_specs=vmem,
        scratch_shapes=[
            pltpu.VMEM((W_SLOTS, width, width), bf16),
            pltpu.VMEM((2, rows, width), f32),
            pltpu.VMEM((2, middle, rows, width), bf16),
            pltpu.VMEM((2, middle, rows, width), bf16),
            dma((2, middle, PIECES)),
            dma((2, middle, PIECES)),
            dma((W_SLOTS,)),
        ],
        compiler_params=pltpu.CompilerParams(
            collective_id=1, has_side_effects=True, vmem_limit_bytes=56 << 20
        ),
    )(gated, tokens, out_weight)


def solution(mesh):
    return jax.shard_map(
        functools.partial(per_device, mesh.shape["chan"]),
        mesh=mesh,
        in_specs=(
            P(("groups", "seq"), "chan"),
            P(),
            P(None, None, "chan"),
            P(None, None, "chan"),
            P(None, "chan"),
            P(None, "chan"),
            P("chan"),
            P("chan", None),
        ),
        out_specs=P(("groups", "seq"), "chan"),
        check_vma=False,
    )
```

```python
import functools

import jax
import jax.numpy as jnp
from jax import lax
from jax.experimental import pallas as pl
from jax.experimental.pallas import tpu as pltpu
from jax.sharding import PartitionSpec as P

EPSILON = 1e-06
MESH = pl.DeviceIdType.MESH
PIECES = 4
OUT_PIECES = 8
W_SLOTS = 4


def ring_position(index, n):
    odd = lax.rem(index, 2)
    return (1 - odd) * lax.div(index, 2) + odd * (n - 1 - lax.div(index, 2))


def ring_index(position, n):
    back = lax.div(position, n // 2)
    return (1 - back) * (2 * position) + back * (2 * (n - 1 - position) + 1)


def greet(peers):
    barrier = pltpu.get_barrier_semaphore()
    for peer in peers:
        pl.semaphore_signal(barrier, inc=1, device_id=peer, device_id_type=MESH)
    pl.semaphore_wait(barrier, len(peers))


def strided(start, size, stride):
    return pl.ds(start, size) if stride == 1 else pl.ds(start, size, stride=stride)


def out_copy(n, pos, w_hbm, w_buf, w_sem, block):
    width = w_buf.shape[1]
    away = n // 2 - lax.div(block + 1, 2)
    odd = lax.rem(block, 2)
    target = ring_index(lax.rem(pos + odd * away + (1 - odd) * (n - away), n), n)
    slot = lax.rem(block, W_SLOTS)
    return pltpu.make_async_copy(
        w_hbm.at[:, pl.ds(pl.multiple_of(target * width, 128), width)],
        w_buf.at[slot],
        w_sem.at[slot],
    )


def front_kernel(
    n, eps, tok_hbm, gain_ref, w_hbm, taps_ref, decay_ref, res_ref, skip_ref, out_hbm, out_ref,
    gated_ref, partial, outgoing, incoming, out_send, out_recv, held, acc, w_buf, scaled, squares, query, signal_rows, pole, residue, skip_rows,
    rim_out, rim_in, state_out, state_in, first_state, send_sem, recv_sem, w_sem, own_sem, pair_send, pair_recv, turn,
):
    rows, width = tok_hbm.shape
    middle = n // 2
    piece = rows // PIECES
    groups = width // 128
    poles = decay_ref.shape[0]
    tap_count = taps_ref.shape[1]
    chunk = min(64, rows)
    tile = min(256, width)
    me = lax.axis_index("chan")
    seq = lax.axis_index("seq")
    pos = ring_position(me, n)
    right = {"chan": ring_index(lax.rem(pos + 1, n), n)}
    left = {"chan": ring_index(lax.rem(pos + n - 1, n), n)}
    partner = {"seq": 1 - seq}
    ahead = (right, left)

    def owner_of(block):
        away = lax.div(block + 1, 2)
        odd = lax.rem(block, 2)
        return ring_index(lax.rem(pos + odd * (n - away) + (1 - odd) * away, n), n)

    def w_copy(g):
        owner = owner_of(lax.div(g, 3))
        slot = lax.rem(g, W_SLOTS)
        return pltpu.make_async_copy(
            w_hbm.at[lax.rem(g, 3), pl.ds(pl.multiple_of(owner * width, 128), width), :],
            w_buf.at[slot],
            w_sem.at[slot],
        )

    def hop(direction, step, part, away):
        shift = pos + n - away if direction == 0 else pos + away
        owner = ring_index(lax.rem(shift, n), n)
        span = pl.ds(part * piece, piece)
        return pltpu.make_async_remote_copy(
            src_ref=held.at[owner, span, :],
            dst_ref=held.at[owner, span, :],
            send_sem=send_sem.at[direction, step, part],
            recv_sem=recv_sem.at[direction, step, part],
            device_id=ahead[direction],
            device_id_type=MESH,
        )

    own = pltpu.make_async_copy(tok_hbm, held.at[me], own_sem)
    own.start()
    for g in range(W_SLOTS):
        w_copy(jnp.int32(g)).start()
    greet((right, left, partner))
    own.wait()

    @pl.when(seq > 0)
    def _():
        pl.semaphore_wait(turn, 1)

    for part in range(PIECES):
        for direction in range(2):
            hop(direction, 0, part, 0).start()

    @pl.loop(0, rows // chunk)
    def _(b):
        r = pl.multiple_of(b * chunk, chunk)
        squares[pl.ds(r, chunk), :] = jnp.zeros((chunk, 128), jnp.float32)
        for i in range(3):
            acc[i, pl.ds(r + 8, chunk), :] = jnp.zeros((chunk, width), jnp.float32)

    for j in range(groups):
        lanes = pl.ds(j * 128, 128)
        pole[strided(j, poles, groups), :] = jnp.exp(decay_ref[:, lanes])
        residue[strided(j, poles, groups), :] = res_ref[:, lanes]
        skip_rows[pl.ds(j, 1), :] = skip_ref[:, lanes]

    def prepare(block):
        owner = owner_of(block)
        gain = gain_ref[:, pl.ds(pl.multiple_of(owner * width, 128), width)]
        small = min(32, rows)

        @pl.loop(0, rows // small)
        def _(b):
            r = pl.multiple_of(b * small, small)
            x = held[owner, pl.ds(r, small), :].astype(jnp.float32)
            scaled[pl.ds(r, small), :] = (x * gain).astype(jnp.bfloat16)
            total = squares[pl.ds(r, small), :]
            for j in range(groups):
                xj = x[:, j * 128 : (j + 1) * 128]
                total = total + xj * xj
            squares[pl.ds(r, small), :] = total

    def multiply(block, i):
        g = block * 3 + i
        slot = lax.rem(g, W_SLOTS)
        w_copy(g).wait()

        @pl.loop(0, width // tile)
        def _(c):
            cols = pl.ds(pl.multiple_of(c * tile, 128), tile)
            acc[i, pl.ds(8, rows), cols] += jnp.dot(
                scaled[...], w_buf[slot, :, cols], preferred_element_type=jnp.float32
            )

        @pl.when(g + W_SLOTS < n * 3)
        def _():
            w_copy(g + W_SLOTS).start()

    def arrive(step, part):
        for direction in range(2):
            hop(direction, step - 1, part, step).wait_recv()
            if part // (PIECES // 2) == direction:
                hop(direction, step, part, step).start()
            else:

                @pl.when(step < middle - 1)
                def _():
                    hop(direction, step, part, step).start()

    def pair_part(step, quarter):
        near = 2 * step - 1
        if quarter == 0:
            prepare(near)
            multiply(near, 0)
            multiply(near, 1)
        elif quarter == 1:
            multiply(near, 2)
        elif quarter == 2:
            prepare(near + 1)
            multiply(near + 1, 0)
            multiply(near + 1, 1)
        else:
            multiply(near + 1, 2)

    for part in range(PIECES):
        arrive(jnp.int32(1), part)
        if part == 0:
            prepare(jnp.int32(0))
        if part < 3:
            multiply(jnp.int32(0), part)

    @pl.loop(2, middle)
    def _(step):
        for part in range(PIECES):
            arrive(step, part)
            pair_part(step - 1, part)

    @pl.when(seq == 0)
    def _():
        pl.semaphore_signal(turn, inc=1, device_id=partner, device_id_type=MESH)

    for part in range(PIECES):
        pair_part(jnp.int32(middle - 1), part)
    for part in range(PIECES):
        hop(part // (PIECES // 2), middle - 1, part, middle).wait_recv()
    prepare(jnp.int32(n - 1))
    for i in range(3):
        multiply(jnp.int32(n - 1), i)
    for block in range(W_SLOTS):
        out_copy(n, pos, out_hbm, w_buf, w_sem, jnp.int32(block)).start()

    @pl.loop(0, rows // chunk)
    def _(b):
        r = pl.multiple_of(b * chunk, chunk)
        mean = jnp.sum(squares[pl.ds(r, chunk), :], axis=1, keepdims=True) / (n * width)
        inv = lax.rsqrt(mean + eps)
        for i in range(3):
            span = pl.ds(r + 8, chunk)
            acc[i, span, :] = (acc[i, span, :] * inv).astype(jnp.bfloat16).astype(jnp.float32)

    rim_out[...] = acc[:, pl.ds(rows, 8), :]
    rim = pltpu.make_async_remote_copy(
        src_ref=rim_out, dst_ref=rim_in, send_sem=pair_send.at[0], recv_sem=pair_recv.at[0],
        device_id=partner, device_id_type=MESH,
    )

    @pl.when(seq == 0)
    def _():
        rim.start()

    @pl.when(seq > 0)
    def _():
        rim.wait_recv()

    acc[:, pl.ds(0, 8), :] = jnp.zeros((3, 8, width), jnp.float32)

    @pl.when(seq > 0)
    def _():
        acc[:, pl.ds(0, 8), :] = rim_in[...]


    @pl.loop(0, groups)
    def _(j):
        lanes = pl.ds(pl.multiple_of(j * 128, 128), 128)

        @pl.loop(0, rows // chunk)
        def _(b):
            r = pl.multiple_of(b * chunk, chunk)
            conv = []
            for i in range(3):
                x = acc[i, pl.ds(r, chunk + 8), lanes]
                total = x[8:, :] * taps_ref[i, pl.ds(0, 1), lanes]
                for tap in range(1, tap_count):
                    shifted = pltpu.roll(x, tap, 0)[8:, :]
                    total = total + shifted * taps_ref[i, pl.ds(tap, 1), lanes]
                conv.append(total)
            query[pl.ds(r, chunk), lanes] = conv[0]
            signal_rows[strided(r * groups + j, chunk, groups), :] = conv[1] * conv[2]

    def row_at(t):
        return pl.ds(pl.multiple_of(t * groups, groups), groups)

    poles_held = [pole[pl.ds(k * groups, groups), :] for k in range(poles)]

    carry = pltpu.make_async_remote_copy(
        src_ref=state_out, dst_ref=state_in, send_sem=pair_send.at[1], recv_sem=pair_recv.at[1],
        device_id=partner, device_id_type=MESH,
    )
    entry_rows = poles * groups

    @pl.when(seq == 0)
    def _():
        first_state[...] = jnp.zeros((entry_rows, 128), jnp.float32)

    @pl.when(seq > 0)
    def _():
        carry.wait_recv()
        first_state[...] = state_in[...]

    res_held = [residue[pl.ds(k * groups, groups), :] for k in range(poles)]
    skip_held = skip_rows[...]

    def with_output(t, state):
        row = signal_rows[row_at(t), :]
        state = tuple(poles_held[k] * state[k] + row for k in range(poles))
        terms = [res_held[k] * state[k] for k in range(poles)]
        while len(terms) > 1:
            terms = [a + b for a, b in zip(terms[::2], terms[1::2])] + terms[len(terms) // 2 * 2 :]
        signal_rows[row_at(t), :] = terms[0] + skip_held * row
        return state

    entry = tuple(first_state[pl.ds(k * groups, groups), :] for k in range(poles))
    last = lax.fori_loop(0, rows, with_output, entry, unroll=4)
    for k in range(poles):
        state_out[pl.ds(k * groups, groups), :] = last[k]

    @pl.when(seq == 0)
    def _():
        carry.start()

    @pl.loop(0, groups)
    def _(j):
        lanes = pl.ds(pl.multiple_of(j * 128, 128), 128)

        @pl.loop(0, rows // chunk)
        def _(b):
            r = pl.multiple_of(b * chunk, chunk)
            long = signal_rows[strided(r * groups + j, chunk, groups), :]
            gated_ref[pl.ds(r, chunk), lanes] = (query[pl.ds(r, chunk), lanes] * long).astype(jnp.bfloat16)

    back_part(
        n, gated_ref, held.at[me], out_hbm, out_ref, w_buf, partial, outgoing, incoming,
        out_send, out_recv, w_sem,
    )

    @pl.when(seq == 0)
    def _():
        rim.wait_send()
        carry.wait_send()

    for part in range(PIECES):
        for direction in range(2):

            @pl.loop(0, middle - 1)
            def _(step):
                hop(direction, step, part, step).wait_send()

        hop(part // (PIECES // 2), middle - 1, part, middle - 1).wait_send()


def back_part(
    n, gated_ref, tok_ref, w_hbm, out_ref, w_buf, partial, outgoing, incoming, send_sem, recv_sem, w_sem
):
    rows, width = tok_ref.shape
    middle = n // 2
    piece = rows // OUT_PIECES
    small = min(32, piece)
    tile = min(256, width)
    me = lax.axis_index("chan")
    pos = ring_position(me, n)
    right = {"chan": ring_index(lax.rem(pos + 1, n), n)}
    left = {"chan": ring_index(lax.rem(pos + n - 1, n), n)}
    ahead = (right, left)

    def w_copy(block):
        return out_copy(n, pos, w_hbm, w_buf, w_sem, block)

    def hop(direction, step, part):
        span = pl.ds(part * piece, piece)
        return pltpu.make_async_remote_copy(
            src_ref=outgoing.at[direction, step, span, :],
            dst_ref=incoming.at[direction, step, span, :],
            send_sem=send_sem.at[direction, step, part],
            recv_sem=recv_sem.at[direction, step, part],
            device_id=ahead[direction],
            device_id_type=MESH,
        )

    def multiply(block, place):
        slot = lax.rem(block, W_SLOTS)
        w_copy(block).wait()

        @pl.loop(0, width // tile)
        def _(c):
            cols = pl.ds(pl.multiple_of(c * tile, 128), tile)
            partial[place, :, cols] = jnp.dot(
                gated_ref[...], w_buf[slot, :, cols], preferred_element_type=jnp.float32
            )

        @pl.when(block + W_SLOTS < n)
        def _():
            w_copy(block + W_SLOTS).start()

    def send(direction, step, part, place, add):
        @pl.loop(0, piece // small)
        def _(b):
            span = pl.ds(pl.multiple_of(part * piece + b * small, small), small)
            total = partial[place, span, :]
            if add:
                total = total + incoming[direction, step - 1, span, :].astype(jnp.float32)
            outgoing[direction, step, span, :] = total.astype(jnp.bfloat16)

        hop(direction, step, part).start()

    def side(part):
        return part // (OUT_PIECES // 2)

    order = [k // 2 + (k % 2) * (OUT_PIECES // 2) for k in range(OUT_PIECES)]
    multiply(jnp.int32(0), 0)
    for part in order:
        send(side(part), 0, part, 0, False)
    for direction in range(2):
        multiply(jnp.int32(1 + direction), direction)
    for direction in range(2):
        for part in range(OUT_PIECES):
            if side(part) != direction:
                send(direction, 1, part, direction, False)
    for part in order:
        hop(side(part), 0, part).wait_recv()
        send(side(part), 1, part, side(part), True)

    @pl.loop(2, middle)
    def _(step):
        for direction in range(2):
            multiply(2 * step - 1 + direction, direction)
        for k in range(OUT_PIECES):
            for direction in range(2):
                part = (k + (1 - direction) * (OUT_PIECES // 2)) % OUT_PIECES
                hop(direction, step - 1, part).wait_recv()
                send(direction, step, part, direction, True)

    multiply(jnp.int32(n - 1), 0)
    for part in range(OUT_PIECES):
        for direction in range(2):
            hop(direction, middle - 1, part).wait_recv()

        @pl.loop(0, piece // small)
        def _(b):
            span = pl.ds(pl.multiple_of(part * piece + b * small, small), small)
            total = partial[0, span, :]
            for direction in range(2):
                total = total + incoming[direction, middle - 1, span, :].astype(jnp.float32)
            out_ref[span, :] = (tok_ref[span, :].astype(jnp.float32) + total).astype(jnp.bfloat16)

    for part in range(OUT_PIECES):
        hop(side(part), 0, part).wait_send()
        for direction in range(2):

            @pl.loop(1, middle)
            def _(step):
                hop(direction, step, part).wait_send()


def per_device(n, tokens, norm_gain, in_weight, short_weight, log_decay, residue, skip, out_weight):
    rows, width = tokens.shape
    groups = width // 128
    poles = log_decay.shape[0]
    middle = n // 2
    vmem = pl.BlockSpec(memory_space=pltpu.VMEM)
    anywhere = pl.BlockSpec(memory_space=pl.ANY)
    f32, bf16 = jnp.float32, jnp.bfloat16
    dma = pltpu.SemaphoreType.DMA
    return pl.pallas_call(
        functools.partial(front_kernel, n, EPSILON),
        out_shape=jax.ShapeDtypeStruct((rows, width), bf16),
        in_specs=[anywhere, vmem, anywhere, vmem, vmem, vmem, vmem, anywhere],
        out_specs=vmem,
        scratch_shapes=[
            pltpu.VMEM((rows, width), bf16),
            pltpu.VMEM((2, rows, width), f32),
            pltpu.VMEM((2, middle, rows, width), bf16),
            pltpu.VMEM((2, middle, rows, width), bf16),
            dma((2, middle, OUT_PIECES)),
            dma((2, middle, OUT_PIECES)),
            pltpu.VMEM((n, rows, width), bf16),
            pltpu.VMEM((3, rows + 8, width), f32),
            pltpu.VMEM((W_SLOTS, width, width), bf16),
            pltpu.VMEM((rows, width), bf16),
            pltpu.VMEM((rows, 128), f32),
            pltpu.VMEM((rows, width), f32),
            pltpu.VMEM((rows * groups, 128), f32),
            pltpu.VMEM((poles * groups, 128), f32),
            pltpu.VMEM((poles * groups, 128), f32),
            pltpu.VMEM((groups, 128), f32),
            pltpu.VMEM((3, 8, width), f32),
            pltpu.VMEM((3, 8, width), f32),
            pltpu.VMEM((poles * groups, 128), f32),
            pltpu.VMEM((poles * groups, 128), f32),
            pltpu.VMEM((poles * groups, 128), f32),
            dma((2, middle, PIECES)),
            dma((2, middle, PIECES)),
            dma((W_SLOTS,)),
            dma,
            dma((2,)),
            dma((2,)),
            pltpu.SemaphoreType.REGULAR,
        ],
        compiler_params=pltpu.CompilerParams(
            collective_id=0, has_side_effects=True, vmem_limit_bytes=56 << 20
        ),
    )(tokens, norm_gain[None, :], in_weight, short_weight, log_decay, residue, skip[None, :], out_weight)


def solution(mesh):
    return jax.shard_map(
        functools.partial(per_device, mesh.shape["chan"]),
        mesh=mesh,
        in_specs=(
            P(("groups", "seq"), "chan"),
            P(),
            P(None, None, "chan"),
            P(None, None, "chan"),
            P(None, "chan"),
            P(None, "chan"),
            P("chan"),
            P("chan", None),
        ),
        out_specs=P(("groups", "seq"), "chan"),
        check_vma=False,
    )
```
